32 devices in a mesh: seq: 4 (over y, x), res: 8 (over z, core).
Axes of the slice: x: 2, y: 2, z: 4, core: 2. Of those that a mesh axis runs over, the one named last changes fastest.
Arguments:
- alignment: float32 [256, 64, 256], P('seq', 'res'), may hold values from -100 to 100
- pair_features: float32 [64, 64, 128], P('seq', 'res'), may hold values from -100 to 100
- outer_gain: float32 [256], replicated, may hold values from 0.5 to 1.5
- w_outer_in: float32 [256, 64], replicated, may hold values from -0.375 to 0.375
- w_outer_out: float32 [1024, 128], replicated, may hold values from -0.1875 to 0.1875
- pair_gain: float32 [128], replicated, may hold values from 0.5 to 1.5
- w_bias: float32 [128, 8], replicated, may hold values from -30 to 30
- row_gain: float32 [256], replicated, may hold values from 0.5 to 1.5
- w_project: float32 [256, 1024], replicated, may hold values from -0.375 to 0.375
- w_output: float32 [256, 256], replicated, may hold values from -0.375 to 0.375
Outputs:
- alignment_out: float32 [256, 64, 256], P('seq', 'res')
- updated_pair_array: float32 [64, 64, 128], P('seq', 'res')
The draws below stay inside these ranges and needn't reach their ends.
All inputs are finite; a program needn't handle non-finite values.
Results may differ from the reference program's by a relative error of at most 0.00018.
Values sent between devices are 32-bit elements; how exact they have to be, the bound alone decides.
A program may use at most 128 MiB of HBM per device.

```python
import math
import jax
import jax.numpy as jnp
from jax import lax

CM = 256
CZ = 128
C = 32
H = 8
SEQS = 256
RES = 64
N_SEQ = 4


def draw_alignment(key, part):
    profile = jax.random.normal(jax.random.fold_in(key, 11), (1, RES, CM), jnp.float32)
    jitter = jax.random.normal(jax.random.fold_in(key, 12), (SEQS, RES, CM), jnp.float32)
    return profile + jitter


def draw_pair_features(key, part):
    jitter = jax.random.normal(jax.random.fold_in(key, 21), (RES, RES, CZ), jnp.float32)
    return jitter


def draw_w_bias(key, part):
    base_map = jax.random.normal(jax.random.fold_in(key, 31), (CZ, H), jnp.float32) / math.sqrt(CZ)
    return base_map


def normal_values(key, shape, width, limit, held_as=jnp.bfloat16):
    drawn = width * jax.random.normal(key, shape, jnp.float32)
    return jnp.clip(drawn, min=-limit, max=limit).astype(held_as)


def setup_inputs(seed: int = 0) -> dict:
    seeds = jax.random.split(jax.random.key(seed), 11)
    alignment = draw_alignment(jax.random.fold_in(seeds[10], 71), 0)
    pair_features = draw_pair_features(jax.random.fold_in(seeds[10], 71), 0)
    outer_gain = jnp.clip(1.0 + 0.1 * jax.random.normal(seeds[2], (CM,), jnp.float32), 0.5, 1.5)
    w_outer_in = normal_values(seeds[3], (CM, 2 * C), CM ** -0.5, 0.375, jnp.float32)
    w_outer_out = normal_values(seeds[4], (C * C, CZ), (C * C) ** -0.5, 0.1875, jnp.float32)
    pair_gain = jnp.clip(1.0 + 0.1 * jax.random.normal(seeds[5], (CZ,), jnp.float32), 0.5, 1.5)
    w_bias = draw_w_bias(jax.random.fold_in(seeds[10], 71), 0)
    row_gain = jnp.clip(1.0 + 0.1 * jax.random.normal(seeds[7], (CM,), jnp.float32), 0.5, 1.5)
    w_project = normal_values(seeds[8], (CM, 4 * CM), CM ** -0.5, 0.375, jnp.float32)
    w_output = normal_values(seeds[9], (CM, CM), CM ** -0.5, 0.375, jnp.float32)
    return {"alignment": alignment, "pair_features": pair_features, "outer_gain": outer_gain, "w_outer_in": w_outer_in, "w_outer_out": w_outer_out, "pair_gain": pair_gain, "w_bias": w_bias, "row_gain": row_gain, "w_project": w_project, "w_output": w_output}


precise = lax.Precision.HIGHEST

def layer_norm(values, scales):
    average = lax.optimization_barrier(jnp.mean(values, axis=-1, keepdims=True))
    centered = values - average
    variance = lax.optimization_barrier(jnp.mean(centered * centered, axis=-1, keepdims=True))
    return centered * lax.rsqrt(variance + 1e-05) * scales

def row_attention(sequence, bias_all, row_gain, w_project, w_output):
    residues, channels = sequence.shape
    head_count = bias_all.shape[0]
    head_size = channels // head_count
    normed_rows = layer_norm(sequence, row_gain)
    projected = jnp.dot(normed_rows, w_project, precision=precise, preferred_element_type=jnp.float32)
    query_map = projected[:, :channels].reshape(residues, head_count, head_size) * head_size ** (-0.5)
    key_map = projected[:, channels:2 * channels].reshape(residues, head_count, head_size)
    value_map = projected[:, 2 * channels:3 * channels].reshape(residues, head_count, head_size)
    gate_map = projected[:, 3 * channels:]
    scores = jnp.einsum('ihd,jhd->hij', query_map, key_map, precision=precise) + bias_all
    weights = jax.nn.softmax(scores, axis=-1)
    mixed_heads = jnp.einsum('hij,jhd->ihd', weights, value_map, precision=precise).reshape(residues, channels)
    gated_out = jax.nn.sigmoid(gate_map) * mixed_heads
    return sequence + jnp.dot(gated_out, w_output, precision=precise, preferred_element_type=jnp.float32)

def reference(alignment, pair_features, outer_gain, w_outer_in, w_outer_out, pair_gain, w_bias, row_gain, w_project, w_output):
    seq_total = alignment.shape[0]
    residues = alignment.shape[1]
    channels = w_outer_in.shape[1] // 2
    normed_rows = layer_norm(alignment, outer_gain)
    both_maps = jnp.einsum('src,cd->sdr', normed_rows, w_outer_in, precision=precise)
    left_maps = both_maps[:, :channels]
    right_maps = both_maps[:, channels:]
    row_block = residues // N_SEQ
    left_blocks = left_maps.reshape(seq_total, channels, N_SEQ, row_block).transpose(2, 0, 1, 3)

    def outer_block(left_part):
        summed = jnp.einsum('sxi,syj->ijxy', left_part, right_maps, precision=precise)
        mean_outer = (summed / seq_total).reshape(row_block, residues, channels * channels)
        return jnp.einsum('ijk,kc->ijc', mean_outer, w_outer_out, precision=precise)
    pair_update = lax.map(outer_block, left_blocks).reshape(residues, residues, w_outer_out.shape[1])
    updated_pair_array = pair_features + pair_update
    bias_all = jnp.einsum('ijc,ch->hij', layer_norm(updated_pair_array, pair_gain), w_bias, precision=precise)

    def attend_one(sequence):
        return row_attention(sequence, bias_all, row_gain, w_project, w_output)
    alignment_out = lax.map(attend_one, alignment)
    return (alignment_out, updated_pair_array)
```

```python
import functools
import jax
import jax.numpy as jnp
from jax import lax
from jax.experimental import pallas as pl
from jax.experimental.pallas import tpu as pltpu
from jax.sharding import PartitionSpec as P

F32 = jnp.float32
BF16 = jnp.bfloat16
MESH = pl.DeviceIdType.MESH
ROWS_COLS = (((1,), (0,)), ((), ()))
ROWS_ROWS = (((1,), (1,)), ((), ()))
COLS_COLS = (((0,), (0,)), ((), ()))
LANES = 128


def split(value):
    high = value.astype(BF16)
    low = (value - high.astype(F32)).astype(BF16)
    return high, low


def dot(a, b, dims=ROWS_COLS):
    return lax.dot_general(a, b, dims, preferred_element_type=F32)


def dot3(a, b, dims=ROWS_COLS):
    return dot(a[0], b[0], dims) + (dot(a[0], b[1], dims) + dot(a[1], b[0], dims))


def layer_norm(values, scales):
    average = jnp.mean(values, axis=-1, keepdims=True)
    centered = values - average
    variance = jnp.mean(centered * centered, axis=-1, keepdims=True)
    return centered * lax.rsqrt(variance + 1e-05) * scales


def kernel(
    n_seq, n_res, heads,
    align_ref, pair_ref, outer_gain_ref, w_in_ref, w_out_ref, pair_gain_ref, w_bias_ref,
    row_gain_ref, w_project_ref, w_output_ref,
    out_ref, pair_out_ref,
    maps, left, right3, rows, w_pair, w_proj, w_outp, update, partial, total, bias,
    q_buf, k_buf, v_buf, gate, done,
    left_s, left_r, rows_s, rows_r, sum_s, sum_r, b1_s, b1_r, b2_s, b2_r, out_s, out_r,
):
    seqs, res, cm = align_ref.shape
    row_block = pair_ref.shape[0]
    cz = pair_ref.shape[2]
    chan = w_in_ref.shape[1] // 2
    group = seqs // n_res
    total_res = res * n_res
    head = cm // heads
    width = res * chan
    tile_rows = row_block * res
    my_seq = lax.axis_index("seq")
    me = lax.axis_index("res")

    barrier = pltpu.get_barrier_semaphore()
    for t in range(1, n_res):
        pl.semaphore_signal(
            barrier, inc=1, device_id=(my_seq, lax.rem(me + t, n_res)), device_id_type=MESH
        )
    for t in range(1, n_seq):
        pl.semaphore_signal(
            barrier, inc=1, device_id=(lax.rem(my_seq + t, n_seq), me), device_id_type=MESH
        )

    def res_copy(src, dst, send, recv, peer):
        return pltpu.make_async_remote_copy(
            src_ref=src, dst_ref=dst, send_sem=send, recv_sem=recv,
            device_id=(my_seq, peer), device_id_type=MESH,
        )

    def seq_copy(src, dst, send, recv, peer):
        return pltpu.make_async_remote_copy(
            src_ref=src, dst_ref=dst, send_sem=send, recv_sem=recv,
            device_id=(peer, me), device_id_type=MESH,
        )

    normed = layer_norm(align_ref[...], outer_gain_ref[...]).reshape(seqs * res, cm)
    maps[:, : 2 * chan] = dot3(split(normed), split(w_in_ref[...]))
    source = lax.broadcasted_iota(jnp.int32, (2 * chan, 2 * width), 0)
    column = lax.broadcasted_iota(jnp.int32, (2 * chan, 2 * width), 1)
    placed = jnp.zeros((seqs, 2 * width), F32)
    for r in range(res):
        target = jnp.where(source < chan, source * res + r, width + r * chan + source - chan)
        pick = jnp.where(column == target, 1.0, 0.0).astype(BF16)
        high, low = split(maps[pl.ds(r, seqs, stride=res), :][:, : 2 * chan])
        placed = placed + (dot(high, pick) + dot(low, pick))
    left[me] = placed[:, :width]
    r_high, r_low = split(placed[:, width:])
    right3[...] = jnp.concatenate([r_high, r_low, r_high], axis=0)

    pl.semaphore_wait(barrier, n_res - 1 + n_seq - 1)

    def send_left(t, c):
        peer = lax.rem(me + t, n_res)
        res_copy(left.at[me], left.at[me], left_s.at[peer], left_r.at[me], peer).start()
        return c

    def rows_copy(peer, slot):
        return res_copy(
            align_ref.at[pl.ds(peer * group, group)],
            rows.at[:, pl.ds(slot * res, res), :],
            rows_s.at[peer], rows_r.at[slot], peer,
        )

    def send_rows(t, c):
        rows_copy(lax.rem(me + t, n_res), me).start()
        return c

    lax.fori_loop(1, n_res, send_left, 0)
    lax.fori_loop(1, n_res, send_rows, 0)
    rows[:, pl.ds(pl.multiple_of(me * res, res), res), :] = align_ref[pl.ds(me * group, group)]

    for ref, wref in ((w_pair, w_out_ref), (w_proj, w_project_ref), (w_outp, w_output_ref)):
        high, low = split(wref[...])
        ref[0] = high
        ref[1] = low

    per = LANES // chan
    lane = lax.broadcasted_iota(jnp.int32, (1, LANES), 1) // chan

    def outer_step(src):
        high, low = split(left[src])
        product = dot(jnp.concatenate([high, high, low], axis=0), right3[...], COLS_COLS)
        parts = product.reshape(chan // per, per, res, width)
        blocks = []
        for j in range(res):
            base = (j // per) * LANES
            acc = None
            for q in range(per):
                piece = parts[:, q, :, base : base + LANES].reshape(-1, LANES)
                shift = ((q - j % per) * chan) % LANES
                if shift:
                    piece = pltpu.roll(piece, shift, 1)
                acc = piece if acc is None else jnp.where(lane == q, piece, acc)
            blocks.append(
                jnp.concatenate([acc[g * res : (g + 1) * res] for g in range(chan // per)], axis=1)
            )
        flat = jnp.concatenate(blocks, axis=0)
        update[pl.ds(pl.multiple_of(src * res * res, res * res), res * res), :] = dot3(
            split(flat), (w_pair[0], w_pair[1])
        )

    def outer_loop(t, c):
        src = lax.rem(me + n_res - t, n_res)
        @pl.when(t > 0)
        def _():
            res_copy(left.at[me], left.at[src], left_s.at[src], left_r.at[src], src).wait_recv()
        outer_step(src)
        return c

    lax.fori_loop(0, n_res, outer_loop, 0)

    def sum_copy(peer, slot):
        return seq_copy(
            update.at[pl.ds(pl.multiple_of(peer * tile_rows, tile_rows), tile_rows)],
            partial.at[slot], sum_s.at[peer], sum_r.at[slot], peer,
        )

    for t in range(1, n_seq):
        sum_copy(lax.rem(my_seq + t, n_seq), my_seq).start()
    summed = update[pl.ds(pl.multiple_of(my_seq * tile_rows, tile_rows), tile_rows), :]
    for t in range(1, n_seq):
        src = lax.rem(my_seq + n_seq - t, n_seq)
        sum_copy(src, src).wait_recv()
        summed = summed + partial[src]
    total[...] = summed * (1.0 / (seqs * n_seq))

    lane_row = lax.broadcasted_iota(jnp.int32, (res, heads * row_block), 1) % row_block
    expand_h = lax.broadcasted_iota(jnp.int32, (heads, heads * row_block), 0)
    expand_l = lax.broadcasted_iota(jnp.int32, (heads, heads * row_block), 1)
    expand = jnp.where(expand_l // row_block == expand_h, 1.0, 0.0)
    w_rep = lax.dot_general(
        w_bias_ref[...], expand, ROWS_COLS,
        precision=lax.Precision.HIGHEST, preferred_element_type=F32,
    )
    tiles = []
    for i in range(row_block):
        start = (i // res) * res * res + i % res
        tile = pair_ref[i] + total[pl.ds(start, res, stride=res), :]
        pair_out_ref[i] = tile
        tiles.append(layer_norm(tile, pair_gain_ref[...]))
    spread = lax.dot_general(
        jnp.concatenate(tiles, axis=0), w_rep, ROWS_COLS,
        precision=lax.Precision.HIGHEST, preferred_element_type=F32,
    )
    tile_bias = jnp.zeros((res, heads * row_block), F32)
    for i in range(row_block):
        tile_bias = jnp.where(lane_row == i, spread[i * res : (i + 1) * res], tile_bias)
    bias[my_seq, pl.ds(pl.multiple_of(me * res, res), res), :] = tile_bias

    def bias_copy(peer, slot):
        return res_copy(
            bias.at[my_seq, pl.ds(pl.multiple_of(me * res, res), res)],
            bias.at[my_seq, pl.ds(pl.multiple_of(slot * res, res), res)],
            b1_s.at[peer], b1_r.at[slot], peer,
        )

    def send_bias(t, c):
        bias_copy(lax.rem(me + t, n_res), me).start()
        return c

    lax.fori_loop(1, n_res, send_bias, 0)

    def wait_rows(t, c):
        src = lax.rem(me + n_res - t, n_res)
        rows_copy(src, src).wait_recv()
        return c

    lax.fori_loop(1, n_res, wait_rows, 0)

    def project(s, c):
        parts = split(layer_norm(rows[s], row_gain_ref[...]))
        mapped = dot3(parts, (w_proj[0], w_proj[1]))
        for buf, k in ((q_buf, 0), (k_buf, 1), (v_buf, 2)):
            value = mapped[:, k * cm : (k + 1) * cm]
            if k == 0:
                value = value * head ** (-0.5)
            high, low = split(value)
            buf[0, s] = high
            buf[1, s] = low
        gate[s] = jax.nn.sigmoid(mapped[:, 3 * cm :])
        return c

    half = group // 2
    lax.fori_loop(0, half, project, 0)

    def wait_bias(t, c):
        src = lax.rem(me + n_res - t, n_res)
        bias_copy(src, src).wait_recv()
        return c

    lax.fori_loop(1, n_res, wait_bias, 0)

    def bias2_copy(peer, slot):
        return seq_copy(bias.at[my_seq], bias.at[slot], b2_s.at[peer], b2_r.at[slot], peer)

    for t in range(1, n_seq):
        bias2_copy(lax.rem(my_seq + t, n_seq), my_seq).start()
    lax.fori_loop(half, group, project, 0)
    for t in range(1, n_seq):
        src = lax.rem(my_seq + n_seq - t, n_seq)
        bias2_copy(src, src).wait_recv()

    channel_head = lax.broadcasted_iota(jnp.int32, (row_block, cm), 1) // head

    def out_copy(s, peer, slot, to):
        return res_copy(
            done.at[s, pl.ds(pl.multiple_of(peer * res, res), res)],
            out_ref.at[slot * group + s],
            out_s.at[s, peer], out_r.at[s, slot], to,
        )

    def attend(s, c):
        keys = (k_buf[0, s], k_buf[1, s])
        v_high, v_low = v_buf[0, s], v_buf[1, s]
        values3 = jnp.concatenate([v_high, v_low, v_high], axis=0)
        mixed = []
        for a in range(n_seq):
            stacked = []
            for k in range(2):
                block = q_buf[k, s, a * row_block : (a + 1) * row_block, :]
                stacked.append(
                    jnp.concatenate(
                        [jnp.where(channel_head == h, block, jnp.zeros_like(block))
                         for h in range(heads)], axis=0)
                )
            scores = dot3(keys, stacked, ROWS_ROWS) + bias[a]
            peak = jnp.max(scores, axis=0, keepdims=True)
            powers = jnp.exp(scores - peak)
            weights = powers / jnp.sum(powers, axis=0, keepdims=True)
            p_high, p_low = split(weights)
            blended = dot(jnp.concatenate([p_high, p_high, p_low], axis=0), values3, COLS_COLS)
            acc = blended[:row_block]
            for h in range(1, heads):
                acc = jnp.where(
                    channel_head == h, blended[h * row_block : (h + 1) * row_block], acc
                )
            mixed.append(acc)
        gated = gate[s] * jnp.concatenate(mixed, axis=0)
        done[s] = rows[s] + dot3(split(gated), (w_outp[0], w_outp[1]))
        out_ref[me * group + s] = done[s, pl.ds(pl.multiple_of(me * res, res), res), :]

        def send_out(t, d):
            peer = lax.rem(me + t, n_res)
            out_copy(s, peer, me, peer).start()
            return d

        lax.fori_loop(1, n_res, send_out, 0)
        return c

    lax.fori_loop(0, group, attend, 0)

    def finish(t, c):
        src = lax.rem(me + n_res - t, n_res)

        def finish_one(s, d):
            out_copy(s, src, src, src).wait()
            return d

        lax.fori_loop(0, group, finish_one, 0)
        res_copy(left.at[me], left.at[src], left_s.at[src], left_r.at[src], src).wait_send()
        rows_copy(src, src).wait_send()
        bias_copy(src, src).wait_send()
        return c

    lax.fori_loop(1, n_res, finish, 0)
    for t in range(1, n_seq):
        src = lax.rem(my_seq + n_seq - t, n_seq)
        sum_copy(src, src).wait_send()
        bias2_copy(src, src).wait_send()


def on_device(n_seq, n_res, *args):
    align, pair, _, w_in, w_out, _, w_bias, _, w_project, w_output = args
    seqs, res, cm = align.shape
    row_block, _, cz = pair.shape
    heads = w_bias.shape[1]
    chan = w_in.shape[1] // 2
    group = seqs // n_res
    total_res = res * n_res
    width = res * chan
    vmem = pl.BlockSpec(memory_space=pltpu.VMEM)
    dma = pltpu.SemaphoreType.DMA
    scratch = [
        pltpu.VMEM((seqs * res, LANES), F32),
        pltpu.VMEM((n_res, seqs, width), F32),
        pltpu.VMEM((3 * seqs, width), BF16),
        pltpu.VMEM((group, total_res, cm), F32),
        pltpu.VMEM((2,) + w_out.shape, BF16),
        pltpu.VMEM((2,) + w_project.shape, BF16),
        pltpu.VMEM((2,) + w_output.shape, BF16),
        pltpu.VMEM((total_res * res, cz), F32),
        pltpu.VMEM((n_seq, row_block * res, cz), F32),
        pltpu.VMEM((row_block * res, cz), F32),
        pltpu.VMEM((n_seq, total_res, heads * row_block), F32),
        pltpu.VMEM((2, group, total_res, cm), BF16),
        pltpu.VMEM((2, group, total_res, cm), BF16),
        pltpu.VMEM((2, group, total_res, cm), BF16),
        pltpu.VMEM((group, total_res, cm), F32),
        pltpu.VMEM((group, total_res, cm), F32),
        dma((n_res,)), dma((n_res,)), dma((n_res,)), dma((n_res,)),
        dma((n_seq,)), dma((n_seq,)), dma((n_res,)), dma((n_res,)),
        dma((n_seq,)), dma((n_seq,)), dma((group, n_res)), dma((group, n_res)),
    ]
    vectors = [a.reshape(1, -1) if a.ndim == 1 else a for a in args]
    return pl.pallas_call(
        functools.partial(kernel, n_seq, n_res, heads),
        out_shape=(
            jax.ShapeDtypeStruct(align.shape, F32),
            jax.ShapeDtypeStruct(pair.shape, F32),
        ),
        in_specs=[vmem] * len(args),
        out_specs=(vmem, vmem),
        scratch_shapes=scratch,
        compiler_params=pltpu.CompilerParams(
            collective_id=0, has_side_effects=True, vmem_limit_bytes=60 * 1024 * 1024
        ),
    )(*vectors)


def solution(mesh):
    tiled = P("seq", "res", None)
    return jax.shard_map(
        functools.partial(on_device, mesh.shape["seq"], mesh.shape["res"]),
        mesh=mesh,
        in_specs=(tiled, tiled) + (P(),) * 8,
        out_specs=(tiled, tiled),
        check_vma=False,
    )
```

```python
import functools
import jax
import jax.numpy as jnp
from jax import lax
from jax.experimental import pallas as pl
from jax.experimental.pallas import tpu as pltpu
from jax.sharding import PartitionSpec as P

F32 = jnp.float32
BF16 = jnp.bfloat16
MESH = pl.DeviceIdType.MESH
ROWS_COLS = (((1,), (0,)), ((), ()))
ROWS_ROWS = (((1,), (1,)), ((), ()))
COLS_COLS = (((0,), (0,)), ((), ()))
LANES = 128
PAIR = 2
CHUNK = 4


def split(value):
    high = value.astype(BF16)
    low = (value - high.astype(F32)).astype(BF16)
    return high, low


def dot(a, b, dims=ROWS_COLS):
    return lax.dot_general(a, b, dims, preferred_element_type=F32)


def dot3(a, b, dims=ROWS_COLS):
    return dot(a[0], b[0], dims) + (dot(a[0], b[1], dims) + dot(a[1], b[0], dims))


def layer_norm(values, scales):
    average = jnp.mean(values, axis=-1, keepdims=True)
    centered = values - average
    variance = jnp.mean(centered * centered, axis=-1, keepdims=True)
    return centered * lax.rsqrt(variance + 1e-05) * scales


def kernel(
    n_seq, n_res, heads,
    align_ref, pair_ref, outer_gain_ref, w_in_ref, w_out_ref, pair_gain_ref, w_bias_ref,
    row_gain_ref, w_project_ref, w_output_ref,
    out_ref, pair_out_ref,
    maps, left, right, right3, rows, w_pair, w_proj, w_outp, update, partial, total, bias,
    q_buf, k_buf, v_buf, gate, done, w_out_v, w_project_v, w_output_v,
    left_s, left_r, right_s, right_r, rows_s, rows_r, sum_s, sum_r, bias_s, bias_r,
    out_s, out_r, load_s,
):
    seqs, res, cm = align_ref.shape
    row_block = pair_ref.shape[0]
    cz = pair_ref.shape[2]
    chan = w_in_ref.shape[0] // 2
    group = seqs // n_res
    total_res = res * n_res
    head = cm // heads
    width = res * chan
    devices = n_seq * n_res
    chips = n_res // PAIR
    part_rows = res * res
    my_seq = lax.axis_index("seq")
    me = lax.axis_index("res")

    barrier = pltpu.get_barrier_semaphore()
    mine = my_seq * n_res + me
    core = lax.rem(me, PAIR)
    chip = me // PAIR
    sibling = chip * PAIR + 1 - core

    def greet(t, c):
        other = lax.rem(mine + t, devices)
        pl.semaphore_signal(
            barrier, inc=1, device_id=(other // n_res, lax.rem(other, n_res)), device_id_type=MESH
        )
        return c

    lax.fori_loop(1, devices, greet, 0)
    loads = [
        pltpu.make_async_copy(hbm, held, load_s.at[k])
        for k, (hbm, held) in enumerate(
            ((w_out_ref, w_out_v), (w_project_ref, w_project_v), (w_output_ref, w_output_v))
        )
    ]
    for load in loads:
        load.start()

    def res_copy(src, dst, send, recv, peer):
        return pltpu.make_async_remote_copy(
            src_ref=src, dst_ref=dst, send_sem=send, recv_sem=recv,
            device_id=(my_seq, peer), device_id_type=MESH,
        )

    def any_copy(src, dst, send, recv, seq, peer):
        return pltpu.make_async_remote_copy(
            src_ref=src, dst_ref=dst, send_sem=send, recv_sem=recv,
            device_id=(seq, peer), device_id_type=MESH,
        )

    normed = layer_norm(align_ref[...], outer_gain_ref[...]).reshape(seqs * res, cm)
    maps[:, : 2 * chan] = dot3(split(normed), split(w_in_ref[...]), ROWS_ROWS)
    source = lax.broadcasted_iota(jnp.int32, (2 * chan, 2 * width), 0)
    column = lax.broadcasted_iota(jnp.int32, (2 * chan, 2 * width), 1)
    placed = jnp.zeros((seqs, 2 * width), F32)
    for r in range(res):
        target = jnp.where(source < chan, source * res + r, width + r * chan + source - chan)
        pick = jnp.where(column == target, 1.0, 0.0).astype(BF16)
        high, low = split(maps[pl.ds(r, seqs, stride=res), :][:, : 2 * chan])
        placed = placed + (dot(high, pick) + dot(low, pick))
    left[chip] = placed[:, :width]
    right[core] = placed[:, width:]

    pl.semaphore_wait(barrier, devices - 1)

    def left_copy(to, slot):
        return res_copy(
            left.at[chip], left.at[slot], left_s.at[to], left_r.at[slot], to * PAIR + core
        )

    def send_left(t, c):
        left_copy(lax.rem(chip + t, chips), chip).start()
        return c

    def right_copy(slot):
        return res_copy(
            right.at[core], right.at[slot], right_s.at[0], right_r.at[0], sibling
        )

    right_copy(core).start()
    lax.fori_loop(1, chips, send_left, 0)

    def rows_copy(peer, slot):
        return res_copy(
            align_ref.at[pl.ds(peer * group, group)],
            rows.at[:, pl.ds(slot * res, res), :],
            rows_s.at[peer], rows_r.at[slot], peer,
        )

    def send_rows(t, c):
        rows_copy(lax.rem(me + t, n_res), me).start()
        return c

    lax.fori_loop(1, n_res, send_rows, 0)
    rows[:, pl.ds(pl.multiple_of(me * res, res), res), :] = align_ref[pl.ds(me * group, group)]

    for load in loads:
        load.wait()
    for ref, wref in ((w_pair, w_out_v), (w_proj, w_project_v), (w_outp, w_output_v)):
        high, low = split(wref[...])
        ref[0] = high
        ref[1] = low

    right_copy(1 - core).wait_recv()
    both = jnp.concatenate([right[k] for k in range(PAIR)], axis=1)
    r_high, r_low = split(both)
    right3[...] = jnp.concatenate([r_high, r_low, r_high], axis=0)
    per = LANES // chan
    lane = lax.broadcasted_iota(jnp.int32, (1, LANES), 1) // chan

    def outer_step(src):
        high, low = split(left[src])
        product = dot(jnp.concatenate([high, high, low], axis=0), right3[...], COLS_COLS)
        parts = product.reshape(chan // per, per, res, PAIR * width)
        blocks = []
        for j in range(PAIR * res):
            base = (j // per) * LANES
            acc = None
            for q in range(per):
                piece = parts[:, q, :, base : base + LANES].reshape(-1, LANES)
                shift = ((q - j % per) * chan) % LANES
                if shift:
                    piece = pltpu.roll(piece, shift, 1)
                acc = piece if acc is None else jnp.where(lane == q, piece, acc)
            blocks.append(
                jnp.concatenate([acc[g * res : (g + 1) * res] for g in range(chan // per)], axis=1)
            )
        flat = jnp.concatenate(blocks, axis=0)
        summed_pair = dot3(
            split(flat), (w_pair[0], w_pair[1])
        )
        for k in range(PAIR):
            update[src, k] = summed_pair[k * part_rows : (k + 1) * part_rows]

    def sum_copy(owner, k, slot_seq, slot_core):
        return any_copy(
            update.at[owner, k], partial.at[slot_seq, slot_core],
            sum_s.at[owner, k], sum_r.at[slot_seq, slot_core], owner, chip * PAIR + k,
        )

    def outer_loop(t, c):
        src = lax.rem(chip + chips - t, chips)
        @pl.when(t > 0)
        def _():
            left_copy(src, src).wait_recv()
        outer_step(src)
        for k in range(PAIR):
            @pl.when(jnp.logical_or(src != my_seq, core != k))
            def _():
                sum_copy(src, k, my_seq, core).start()
        return c

    lax.fori_loop(0, chips, outer_loop, 0)

    partial[my_seq, core] = update[my_seq, core]
    for a in range(n_seq):
        for k in range(PAIR):
            @pl.when(jnp.logical_or(a != my_seq, core != k))
            def _():
                sum_copy(a, k, a, k).wait_recv()
    summed = jnp.concatenate(
        [functools.reduce(jnp.add, [partial[a, k] for a in range(n_seq)]) for k in range(PAIR)],
        axis=0,
    )
    total[...] = summed * (1.0 / (seqs * n_seq))

    lane_row = lax.broadcasted_iota(jnp.int32, (res, heads * row_block), 1) % row_block
    expand_h = lax.broadcasted_iota(jnp.int32, (heads, heads * row_block), 0)
    expand_l = lax.broadcasted_iota(jnp.int32, (heads, heads * row_block), 1)
    expand = jnp.where(expand_l // row_block == expand_h, 1.0, 0.0)
    w_rep = lax.dot_general(
        w_bias_ref[...], expand, COLS_COLS,
        precision=lax.Precision.HIGHEST, preferred_element_type=F32,
    )
    tiles = []
    for i in range(row_block):
        start = (i // res) * res * res + i % res
        tile = pair_ref[i] + total[pl.ds(start, res, stride=res), :]
        pair_out_ref[i] = tile
        tiles.append(layer_norm(tile, pair_gain_ref[...]))
    spread = lax.dot_general(
        jnp.concatenate(tiles, axis=0), w_rep, ROWS_COLS,
        precision=lax.Precision.HIGHEST, preferred_element_type=F32,
    )
    tile_bias = jnp.zeros((res, heads * row_block), F32)
    for i in range(row_block):
        tile_bias = jnp.where(lane_row == i, spread[i * res : (i + 1) * res], tile_bias)
    bias[my_seq, pl.ds(pl.multiple_of(me * res, res), res), :] = tile_bias

    def bias_copy(other, slot):
        place = bias.at[slot // n_res, pl.ds(pl.multiple_of(lax.rem(slot, n_res) * res, res), res)]
        own = bias.at[my_seq, pl.ds(pl.multiple_of(me * res, res), res)]
        return any_copy(
            own, place, bias_s.at[other], bias_r.at[slot], other // n_res, lax.rem(other, n_res)
        )

    def send_bias(t, c):
        bias_copy(lax.rem(mine + t, devices), mine).start()
        return c

    lax.fori_loop(1, devices, send_bias, 0)

    def wait_rows(t, c):
        src = lax.rem(me + n_res - t, n_res)
        rows_copy(src, src).wait_recv()
        return c

    lax.fori_loop(1, n_res, wait_rows, 0)

    def project(s, c):
        parts = split(layer_norm(rows[s], row_gain_ref[...]))
        mapped = dot3(parts, (w_proj[0], w_proj[1]))
        for buf, k in ((q_buf, 0), (k_buf, 1), (v_buf, 2)):
            value = mapped[:, k * cm : (k + 1) * cm]
            if k == 0:
                value = value * head ** (-0.5)
            high, low = split(value)
            buf[0, s] = high
            buf[1, s] = low
        gate[s] = jax.nn.sigmoid(mapped[:, 3 * cm :])
        return c

    lax.fori_loop(0, group, project, 0)

    def wait_bias(t, c):
        src = lax.rem(mine + devices - t, devices)
        bias_copy(src, src).wait_recv()
        return c

    lax.fori_loop(1, devices, wait_bias, 0)

    channel_head = lax.broadcasted_iota(jnp.int32, (row_block, cm), 1) // head

    def out_copy(s, peer, slot, to):
        return res_copy(
            done.at[s, pl.ds(pl.multiple_of(peer * res, res), res)],
            out_ref.at[slot * group + s],
            out_s.at[s, peer], out_r.at[s, slot], to,
        )

    def attend(s, c):
        keys = (k_buf[0, s], k_buf[1, s])
        v_high, v_low = v_buf[0, s], v_buf[1, s]
        values3 = jnp.concatenate([v_high, v_low, v_high], axis=0)
        mixed = []
        for a0 in range(0, n_seq, CHUNK):
            chunk = range(a0, min(a0 + CHUNK, n_seq))
            stacked = [
                jnp.concatenate(
                    [jnp.where(channel_head == h, block, jnp.zeros_like(block))
                     for block in [q_buf[k, s, a * row_block : (a + 1) * row_block, :] for a in chunk]
                     for h in range(heads)], axis=0)
                for k in range(2)
            ]
            scores = dot3(keys, stacked, ROWS_ROWS) + jnp.concatenate([bias[a] for a in chunk], axis=1)
            peak = jnp.max(scores, axis=0, keepdims=True)
            powers = jnp.exp(scores - peak)
            weights = powers / jnp.sum(powers, axis=0, keepdims=True)
            p_high, p_low = split(weights)
            blended = dot(jnp.concatenate([p_high, p_high, p_low], axis=0), values3, COLS_COLS)
            for n in range(len(chunk)):
                base = n * heads * row_block
                acc = blended[base : base + row_block]
                for h in range(1, heads):
                    low = base + h * row_block
                    acc = jnp.where(channel_head == h, blended[low : low + row_block], acc)
                mixed.append(acc)
        gated = gate[s] * jnp.concatenate(mixed, axis=0)
        done[s] = rows[s] + dot3(split(gated), (w_outp[0], w_outp[1]))
        out_ref[me * group + s] = done[s, pl.ds(pl.multiple_of(me * res, res), res), :]

        def send_out(t, d):
            peer = lax.rem(me + t, n_res)
            out_copy(s, peer, me, peer).start()
            return d

        lax.fori_loop(1, n_res, send_out, 0)
        return c

    lax.fori_loop(0, group, attend, 0)

    def finish(t, c):
        src = lax.rem(me + n_res - t, n_res)

        def finish_one(s, d):
            out_copy(s, src, src, src).wait()
            return d

        lax.fori_loop(0, group, finish_one, 0)
        rows_copy(src, src).wait_send()
        return c

    lax.fori_loop(1, n_res, finish, 0)

    def finish_left(t, c):
        left_copy(lax.rem(chip + t, chips), chip).wait_send()
        return c

    lax.fori_loop(1, chips, finish_left, 0)
    right_copy(core).wait_send()
    for a in range(n_seq):
        for k in range(PAIR):
            @pl.when(jnp.logical_or(a != my_seq, core != k))
            def _():
                sum_copy(a, k, my_seq, core).wait_send()

    def finish_bias(t, c):
        bias_copy(lax.rem(mine + t, devices), mine).wait_send()
        return c

    lax.fori_loop(1, devices, finish_bias, 0)


def on_device(n_seq, n_res, *args):
    align, pair, _, w_in, w_out, _, w_bias, _, w_project, w_output = args
    seqs, res, cm = align.shape
    row_block, _, cz = pair.shape
    heads = w_bias.shape[1]
    chan = w_in.shape[1] // 2
    assert row_block == PAIR * res and n_res == PAIR * n_seq
    chips = n_res // PAIR
    group = seqs // n_res
    total_res = res * n_res
    width = res * chan
    vmem = pl.BlockSpec(memory_space=pltpu.VMEM)
    dma = pltpu.SemaphoreType.DMA
    scratch = [
        pltpu.VMEM((seqs * res, LANES), F32),
        pltpu.VMEM((chips, seqs, width), F32),
        pltpu.VMEM((PAIR, seqs, width), F32),
        pltpu.VMEM((3 * seqs, PAIR * width), BF16),
        pltpu.VMEM((group, total_res, cm), F32),
        pltpu.VMEM((2,) + w_out.shape, BF16),
        pltpu.VMEM((2,) + w_project.shape, BF16),
        pltpu.VMEM((2,) + w_output.shape, BF16),
        pltpu.VMEM((chips, PAIR, res * res, cz), F32),
        pltpu.VMEM((n_seq, PAIR, res * res, cz), F32),
        pltpu.VMEM((row_block * res, cz), F32),
        pltpu.VMEM((n_seq, total_res, heads * row_block), F32),
        pltpu.VMEM((2, group, total_res, cm), BF16),
        pltpu.VMEM((2, group, total_res, cm), BF16),
        pltpu.VMEM((2, group, total_res, cm), BF16),
        pltpu.VMEM((group, total_res, cm), F32),
        pltpu.VMEM((group, total_res, cm), F32),
        pltpu.VMEM(w_out.shape, F32),
        pltpu.VMEM(w_project.shape, F32),
        pltpu.VMEM(w_output.shape, F32),
        dma((chips,)), dma((chips,)), dma((1,)), dma((1,)), dma((n_res,)), dma((n_res,)),
        dma((n_seq, PAIR)), dma((n_seq, PAIR)), dma((n_seq * n_res,)), dma((n_seq * n_res,)),
        dma((group, n_res)), dma((group, n_res)), dma((3,)),
    ]
    vectors = [a.reshape(1, -1) if a.ndim == 1 else a for a in args]
    vectors[3] = w_in.T
    vectors[6] = w_bias.T
    hbm = pl.BlockSpec(memory_space=pl.ANY)
    return pl.pallas_call(
        functools.partial(kernel, n_seq, n_res, heads),
        out_shape=(
            jax.ShapeDtypeStruct(align.shape, F32),
            jax.ShapeDtypeStruct(pair.shape, F32),
        ),
        in_specs=[hbm if k in (4, 8, 9) else vmem for k in range(len(args))],
        out_specs=(vmem, vmem),
        scratch_shapes=scratch,
        compiler_params=pltpu.CompilerParams(
            collective_id=0, has_side_effects=True, vmem_limit_bytes=60 * 1024 * 1024
        ),
    )(*vectors)


def solution(mesh):
    tiled = P("seq", "res", None)
    return jax.shard_map(
        functools.partial(on_device, mesh.shape["seq"], mesh.shape["res"]),
        mesh=mesh,
        in_specs=(tiled, tiled) + (P(),) * 8,
        out_specs=(tiled, tiled),
        check_vma=False,
    )
```

```python
import functools
import jax
import jax.numpy as jnp
from jax import lax
from jax.experimental import pallas as pl
from jax.experimental.pallas import tpu as pltpu
from jax.sharding import PartitionSpec as P

F32 = jnp.float32
BF16 = jnp.bfloat16
MESH = pl.DeviceIdType.MESH
ROWS_COLS = (((1,), (0,)), ((), ()))
ROWS_ROWS = (((1,), (1,)), ((), ()))
COLS_COLS = (((0,), (0,)), ((), ()))
LANES = 128
PAIR = 2
CHUNK = 4


def split(value):
    high = value.astype(BF16)
    low = (value - high.astype(F32)).astype(BF16)
    return high, low


def dot(a, b, dims=ROWS_COLS):
    return lax.dot_general(a, b, dims, preferred_element_type=F32)


def dot3(a, b, dims=ROWS_COLS):
    return dot(a[0], b[0], dims) + (dot(a[0], b[1], dims) + dot(a[1], b[0], dims))


def layer_norm(values, scales):
    average = jnp.mean(values, axis=-1, keepdims=True)
    centered = values - average
    variance = jnp.mean(centered * centered, axis=-1, keepdims=True)
    return centered * lax.rsqrt(variance + 1e-05) * scales


def kernel(
    n_seq, n_res, heads,
    align_ref, pair_ref, outer_gain_ref, w_in_ref, w_out_ref, pair_gain_ref, w_bias_ref,
    row_gain_ref, w_project_ref, w_output_ref,
    out_ref, pair_out_ref,
    maps, left, right, right3, rows, w_pair, w_proj, w_outp, update, partial, total, bias,
    q_buf, k_buf, v_buf, gate, done, w_out_v, w_project_v, w_output_v,
    left_s, left_r, right_s, right_r, rows_s, rows_r, sum_s, sum_r, bias_s, bias_r,
    out_s, out_r, load_s,
):
    seqs, res, cm = align_ref.shape
    row_block = pair_ref.shape[0]
    cz = pair_ref.shape[2]
    chan = w_in_ref.shape[0] // 2
    group = seqs // n_res
    total_res = res * n_res
    head = cm // heads
    width = res * chan
    devices = n_seq * n_res
    chips = n_res // PAIR
    part_rows = res * res
    my_seq = lax.axis_index("seq")
    me = lax.axis_index("res")

    barrier = pltpu.get_barrier_semaphore()
    mine = my_seq * n_res + me
    core = lax.rem(me, PAIR)
    chip = me // PAIR
    sibling = chip * PAIR + 1 - core

    def greet(t, c):
        other = lax.rem(mine + t, devices)
        pl.semaphore_signal(
            barrier, inc=1, device_id=(other // n_res, lax.rem(other, n_res)), device_id_type=MESH
        )
        return c

    lax.fori_loop(1, devices, greet, 0)
    loads = [
        pltpu.make_async_copy(hbm, held, load_s.at[k])
        for k, (hbm, held) in enumerate(
            ((w_out_ref, w_out_v), (w_project_ref, w_project_v), (w_output_ref, w_output_v))
        )
    ]
    for load in loads:
        load.start()

    def res_copy(src, dst, send, recv, peer):
        return pltpu.make_async_remote_copy(
            src_ref=src, dst_ref=dst, send_sem=send, recv_sem=recv,
            device_id=(my_seq, peer), device_id_type=MESH,
        )

    def any_copy(src, dst, send, recv, seq, peer):
        return pltpu.make_async_remote_copy(
            src_ref=src, dst_ref=dst, send_sem=send, recv_sem=recv,
            device_id=(seq, peer), device_id_type=MESH,
        )

    normed = layer_norm(align_ref[...], outer_gain_ref[...]).reshape(seqs * res, cm)
    half = group // 2

    def rows_copy(peer, slot, part):
        return res_copy(
            align_ref.at[pl.ds(peer * group + part * half, half)],
            rows.at[pl.ds(part * half, half), pl.ds(pl.multiple_of(slot * res, res), res), :],
            rows_s.at[part, peer], rows_r.at[part, slot], peer,
        )

    def send_rows(part):
        def send(t, c):
            rows_copy(lax.rem(me + t, n_res), me, part).start()
            return c

        lax.fori_loop(1, n_res, send, 0)

    pl.semaphore_wait(barrier, devices - 1)
    send_rows(0)
    maps[:, : 2 * chan] = dot3(split(normed), split(w_in_ref[...]), ROWS_ROWS)
    source = lax.broadcasted_iota(jnp.int32, (2 * chan, 2 * width), 0)
    column = lax.broadcasted_iota(jnp.int32, (2 * chan, 2 * width), 1)
    placed = jnp.zeros((seqs, 2 * width), F32)
    for r in range(res):
        target = jnp.where(source < chan, source * res + r, width + r * chan + source - chan)
        pick = jnp.where(column == target, 1.0, 0.0).astype(BF16)
        high, low = split(maps[pl.ds(r, seqs, stride=res), :][:, : 2 * chan])
        placed = placed + (dot(high, pick) + dot(low, pick))
    left[chip] = placed[:, :width]
    right[core] = placed[:, width:]

    def left_copy(to, slot):
        return res_copy(
            left.at[chip], left.at[slot], left_s.at[to], left_r.at[slot], to * PAIR + core
        )

    def send_left(t, c):
        left_copy(lax.rem(chip + t, chips), chip).start()
        return c

    def right_copy(slot):
        return res_copy(
            right.at[core], right.at[slot], right_s.at[0], right_r.at[0], sibling
        )

    right_copy(core).start()
    lax.fori_loop(1, chips, send_left, 0)

    send_rows(1)
    rows[:, pl.ds(pl.multiple_of(me * res, res), res), :] = align_ref[pl.ds(me * group, group)]

    for load in loads:
        load.wait()
    for ref, wref in ((w_pair, w_out_v), (w_proj, w_project_v), (w_outp, w_output_v)):
        high, low = split(wref[...])
        ref[0] = high
        ref[1] = low

    right_copy(1 - core).wait_recv()
    both = jnp.concatenate([right[k] for k in range(PAIR)], axis=1)
    r_high, r_low = split(both)
    right3[...] = jnp.concatenate([r_high, r_low, r_high], axis=0)
    per = LANES // chan
    lane = lax.broadcasted_iota(jnp.int32, (1, LANES), 1) // chan

    def outer_step(src):
        high, low = split(left[src])
        product = dot(jnp.concatenate([high, high, low], axis=0), right3[...], COLS_COLS)
        parts = product.reshape(chan // per, per, res, PAIR * width)
        blocks = []
        for j in range(PAIR * res):
            base = (j // per) * LANES
            acc = None
            for q in range(per):
                piece = parts[:, q, :, base : base + LANES].reshape(-1, LANES)
                shift = ((q - j % per) * chan) % LANES
                if shift:
                    piece = pltpu.roll(piece, shift, 1)
                acc = piece if acc is None else jnp.where(lane == q, piece, acc)
            blocks.append(
                jnp.concatenate([acc[g * res : (g + 1) * res] for g in range(chan // per)], axis=1)
            )
        flat = jnp.concatenate(blocks, axis=0)
        summed_pair = dot3(
            split(flat), (w_pair[0], w_pair[1])
        )
        for k in range(PAIR):
            update[src, k] = summed_pair[k * part_rows : (k + 1) * part_rows]

    def sum_copy(owner, k, slot_seq, slot_core):
        return any_copy(
            update.at[owner, k], partial.at[slot_seq, slot_core],
            sum_s.at[owner, k], sum_r.at[slot_seq, slot_core], owner, chip * PAIR + k,
        )

    def outer_loop(t, c):
        src = lax.rem(chip + chips - t, chips)
        @pl.when(t > 0)
        def _():
            left_copy(src, src).wait_recv()
        outer_step(src)
        for k in range(PAIR):
            @pl.when(jnp.logical_or(src != my_seq, core != k))
            def _():
                sum_copy(src, k, my_seq, core).start()
        return c

    lax.fori_loop(0, chips, outer_loop, 0)

    def project(s, c):
        parts = split(layer_norm(rows[s], row_gain_ref[...]))
        mapped = dot3(parts, (w_proj[0], w_proj[1]))
        for buf, k in ((q_buf, 0), (k_buf, 1), (v_buf, 2)):
            value = mapped[:, k * cm : (k + 1) * cm]
            if k == 0:
                value = value * head ** (-0.5)
            high, low = split(value)
            buf[0, s] = high
            buf[1, s] = low
        gate[s] = jax.nn.sigmoid(mapped[:, 3 * cm :])
        return c

    def project_part(part):
        def wait_rows(t, c):
            src = lax.rem(me + n_res - t, n_res)
            rows_copy(src, src, part).wait_recv()
            return c

        lax.fori_loop(1, n_res, wait_rows, 0)
        lax.fori_loop(part * half, (part + 1) * half, project, 0)

    project_part(0)

    partial[my_seq, core] = update[my_seq, core]
    for a in range(n_seq):
        for k in range(PAIR):
            @pl.when(jnp.logical_or(a != my_seq, core != k))
            def _():
                sum_copy(a, k, a, k).wait_recv()
    summed = jnp.concatenate(
        [functools.reduce(jnp.add, [partial[a, k] for a in range(n_seq)]) for k in range(PAIR)],
        axis=0,
    )
    total[...] = summed * (1.0 / (seqs * n_seq))

    lane_row = lax.broadcasted_iota(jnp.int32, (res, heads * row_block), 1) % row_block
    expand_h = lax.broadcasted_iota(jnp.int32, (heads, heads * row_block), 0)
    expand_l = lax.broadcasted_iota(jnp.int32, (heads, heads * row_block), 1)
    expand = jnp.where(expand_l // row_block == expand_h, 1.0, 0.0)
    w_rep = lax.dot_general(
        w_bias_ref[...], expand, COLS_COLS,
        precision=lax.Precision.HIGHEST, preferred_element_type=F32,
    )
    tiles = []
    for i in range(row_block):
        start = (i // res) * res * res + i % res
        tile = pair_ref[i] + total[pl.ds(start, res, stride=res), :]
        pair_out_ref[i] = tile
        tiles.append(layer_norm(tile, pair_gain_ref[...]))
    spread = lax.dot_general(
        jnp.concatenate(tiles, axis=0), w_rep, ROWS_COLS,
        precision=lax.Precision.HIGHEST, preferred_element_type=F32,
    )
    tile_bias = jnp.zeros((res, heads * row_block), F32)
    for i in range(row_block):
        tile_bias = jnp.where(lane_row == i, spread[i * res : (i + 1) * res], tile_bias)
    bias[my_seq, pl.ds(pl.multiple_of(me * res, res), res), :] = tile_bias

    def bias_copy(other, slot):
        place = bias.at[slot // n_res, pl.ds(pl.multiple_of(lax.rem(slot, n_res) * res, res), res)]
        own = bias.at[my_seq, pl.ds(pl.multiple_of(me * res, res), res)]
        return any_copy(
            own, place, bias_s.at[other], bias_r.at[slot], other // n_res, lax.rem(other, n_res)
        )

    def send_bias(t, c):
        bias_copy(lax.rem(mine + t, devices), mine).start()
        return c

    lax.fori_loop(1, devices, send_bias, 0)

    project_part(1)

    def wait_bias(t, c):
        src = lax.rem(mine + devices - t, devices)
        bias_copy(src, src).wait_recv()
        return c

    lax.fori_loop(1, devices, wait_bias, 0)

    channel_head = lax.broadcasted_iota(jnp.int32, (row_block, cm), 1) // head

    def out_copy(s, peer, slot, to):
        return res_copy(
            done.at[s, pl.ds(pl.multiple_of(peer * res, res), res)],
            out_ref.at[slot * group + s],
            out_s.at[s, peer], out_r.at[s, slot], to,
        )

    def attend(s, c):
        keys = (k_buf[0, s], k_buf[1, s])
        v_high, v_low = v_buf[0, s], v_buf[1, s]
        values3 = jnp.concatenate([v_high, v_low, v_high], axis=0)
        mixed = []
        for a0 in range(0, n_seq, CHUNK):
            chunk = range(a0, min(a0 + CHUNK, n_seq))
            stacked = [
                jnp.concatenate(
                    [jnp.where(channel_head == h, block, jnp.zeros_like(block))
                     for block in [q_buf[k, s, a * row_block : (a + 1) * row_block, :] for a in chunk]
                     for h in range(heads)], axis=0)
                for k in range(2)
            ]
            scores = dot3(keys, stacked, ROWS_ROWS) + jnp.concatenate([bias[a] for a in chunk], axis=1)
            peak = jnp.max(scores, axis=0, keepdims=True)
            powers = jnp.exp(scores - peak)
            weights = powers / jnp.sum(powers, axis=0, keepdims=True)
            p_high, p_low = split(weights)
            blended = dot(jnp.concatenate([p_high, p_high, p_low], axis=0), values3, COLS_COLS)
            for n in range(len(chunk)):
                base = n * heads * row_block
                acc = blended[base : base + row_block]
                for h in range(1, heads):
                    low = base + h * row_block
                    acc = jnp.where(channel_head == h, blended[low : low + row_block], acc)
                mixed.append(acc)
        gated = gate[s] * jnp.concatenate(mixed, axis=0)
        done[s] = rows[s] + dot3(split(gated), (w_outp[0], w_outp[1]))
        out_ref[me * group + s] = done[s, pl.ds(pl.multiple_of(me * res, res), res), :]

        def send_out(t, d):
            peer = lax.rem(me + t, n_res)
            out_copy(s, peer, me, peer).start()
            return d

        lax.fori_loop(1, n_res, send_out, 0)
        return c

    lax.fori_loop(0, group, attend, 0)

    def finish(t, c):
        src = lax.rem(me + n_res - t, n_res)

        def finish_one(s, d):
            out_copy(s, src, src, src).wait()
            return d

        lax.fori_loop(0, group, finish_one, 0)
        rows_copy(src, src, 0).wait_send()
        rows_copy(src, src, 1).wait_send()
        return c

    lax.fori_loop(1, n_res, finish, 0)

    def finish_left(t, c):
        left_copy(lax.rem(chip + t, chips), chip).wait_send()
        return c

    lax.fori_loop(1, chips, finish_left, 0)
    right_copy(core).wait_send()
    for a in range(n_seq):
        for k in range(PAIR):
            @pl.when(jnp.logical_or(a != my_seq, core != k))
            def _():
                sum_copy(a, k, my_seq, core).wait_send()

    def finish_bias(t, c):
        bias_copy(lax.rem(mine + t, devices), mine).wait_send()
        return c

    lax.fori_loop(1, devices, finish_bias, 0)


def on_device(n_seq, n_res, *args):
    align, pair, _, w_in, w_out, _, w_bias, _, w_project, w_output = args
    seqs, res, cm = align.shape
    row_block, _, cz = pair.shape
    heads = w_bias.shape[1]
    chan = w_in.shape[1] // 2
    assert row_block == PAIR * res and n_res == PAIR * n_seq
    chips = n_res // PAIR
    group = seqs // n_res
    assert group % 2 == 0
    total_res = res * n_res
    width = res * chan
    vmem = pl.BlockSpec(memory_space=pltpu.VMEM)
    dma = pltpu.SemaphoreType.DMA
    scratch = [
        pltpu.VMEM((seqs * res, LANES), F32),
        pltpu.VMEM((chips, seqs, width), F32),
        pltpu.VMEM((PAIR, seqs, width), F32),
        pltpu.VMEM((3 * seqs, PAIR * width), BF16),
        pltpu.VMEM((group, total_res, cm), F32),
        pltpu.VMEM((2,) + w_out.shape, BF16),
        pltpu.VMEM((2,) + w_project.shape, BF16),
        pltpu.VMEM((2,) + w_output.shape, BF16),
        pltpu.VMEM((chips, PAIR, res * res, cz), F32),
        pltpu.VMEM((n_seq, PAIR, res * res, cz), F32),
        pltpu.VMEM((row_block * res, cz), F32),
        pltpu.VMEM((n_seq, total_res, heads * row_block), F32),
        pltpu.VMEM((2, group, total_res, cm), BF16),
        pltpu.VMEM((2, group, total_res, cm), BF16),
        pltpu.VMEM((2, group, total_res, cm), BF16),
        pltpu.VMEM((group, total_res, cm), F32),
        pltpu.VMEM((group, total_res, cm), F32),
        pltpu.VMEM(w_out.shape, F32),
        pltpu.VMEM(w_project.shape, F32),
        pltpu.VMEM(w_output.shape, F32),
        dma((chips,)), dma((chips,)), dma((1,)), dma((1,)), dma((2, n_res)), dma((2, n_res)),
        dma((n_seq, PAIR)), dma((n_seq, PAIR)), dma((n_seq * n_res,)), dma((n_seq * n_res,)),
        dma((group, n_res)), dma((group, n_res)), dma((3,)),
    ]
    vectors = [a.reshape(1, -1) if a.ndim == 1 else a for a in args]
    vectors[3] = w_in.T
    vectors[6] = w_bias.T
    hbm = pl.BlockSpec(memory_space=pl.ANY)
    return pl.pallas_call(
        functools.partial(kernel, n_seq, n_res, heads),
        out_shape=(
            jax.ShapeDtypeStruct(align.shape, F32),
            jax.ShapeDtypeStruct(pair.shape, F32),
        ),
        in_specs=[hbm if k in (4, 8, 9) else vmem for k in range(len(args))],
        out_specs=(vmem, vmem),
        scratch_shapes=scratch,
        compiler_params=pltpu.CompilerParams(
            collective_id=0, has_side_effects=True, vmem_limit_bytes=60 * 1024 * 1024
        ),
    )(*vectors)


def solution(mesh):
    tiled = P("seq", "res", None)
    return jax.shard_map(
        functools.partial(on_device, mesh.shape["seq"], mesh.shape["res"]),
        mesh=mesh,
        in_specs=(tiled, tiled) + (P(),) * 8,
        out_specs=(tiled, tiled),
        check_vma=False,
    )
```

```python
import functools
import jax
import jax.numpy as jnp
from jax import lax
from jax.experimental import pallas as pl
from jax.experimental.pallas import tpu as pltpu
from jax.sharding import PartitionSpec as P

F32 = jnp.float32
BF16 = jnp.bfloat16
MESH = pl.DeviceIdType.MESH
ROWS_COLS = (((1,), (0,)), ((), ()))
ROWS_ROWS = (((1,), (1,)), ((), ()))
COLS_COLS = (((0,), (0,)), ((), ()))
LANES = 128
PAIR = 2
CHUNK = 4


def split(value):
    high = value.astype(BF16)
    low = (value - high.astype(F32)).astype(BF16)
    return high, low


def dot(a, b, dims=ROWS_COLS):
    return lax.dot_general(a, b, dims, preferred_element_type=F32)


def dot3(a, b, dims=ROWS_COLS):
    return dot(a[0], b[0], dims) + (dot(a[0], b[1], dims) + dot(a[1], b[0], dims))


def layer_norm(values, scales):
    average = jnp.mean(values, axis=-1, keepdims=True)
    centered = values - average
    variance = jnp.mean(centered * centered, axis=-1, keepdims=True)
    return centered * lax.rsqrt(variance + 1e-05) * scales


def kernel(
    n_seq, n_res, heads,
    align_ref, pair_ref, outer_gain_ref, w_in_ref, w_out_ref, pair_gain_ref, w_bias_ref,
    row_gain_ref, w_project_ref, w_output_ref,
    out_ref, pair_out_ref,
    maps, left, right, right3, rows, w_pair, w_proj, w_outp, update, partial, total, bias,
    q_buf, k_buf, v_buf, gate, done, w_out_v, w_project_v, w_output_v,
    left_s, left_r, right_s, right_r, rows_s, rows_r, sum_s, sum_r, bias_s, bias_r,
    out_s, out_r, own_s, load_s,
):
    seqs, res, cm = align_ref.shape
    row_block = pair_ref.shape[0]
    cz = pair_ref.shape[2]
    chan = w_in_ref.shape[0] // 2
    group = seqs // n_res
    total_res = res * n_res
    head = cm // heads
    width = res * chan
    devices = n_seq * n_res
    chips = n_res // PAIR
    part_rows = res * res
    my_seq = lax.axis_index("seq")
    me = lax.axis_index("res")

    barrier = pltpu.get_barrier_semaphore()
    mine = my_seq * n_res + me
    core = lax.rem(me, PAIR)
    chip = me // PAIR
    sibling = chip * PAIR + 1 - core

    def greet(t, c):
        other = lax.rem(mine + t, devices)
        pl.semaphore_signal(
            barrier, inc=1, device_id=(other // n_res, lax.rem(other, n_res)), device_id_type=MESH
        )
        return c

    lax.fori_loop(1, devices, greet, 0)
    loads = [
        pltpu.make_async_copy(hbm, held, load_s.at[k])
        for k, (hbm, held) in enumerate(
            ((w_out_ref, w_out_v), (w_project_ref, w_project_v), (w_output_ref, w_output_v))
        )
    ]
    for load in loads:
        load.start()

    def res_copy(src, dst, send, recv, peer):
        return pltpu.make_async_remote_copy(
            src_ref=src, dst_ref=dst, send_sem=send, recv_sem=recv,
            device_id=(my_seq, peer), device_id_type=MESH,
        )

    def any_copy(src, dst, send, recv, seq, peer):
        return pltpu.make_async_remote_copy(
            src_ref=src, dst_ref=dst, send_sem=send, recv_sem=recv,
            device_id=(seq, peer), device_id_type=MESH,
        )

    normed = layer_norm(align_ref[...], outer_gain_ref[...]).reshape(seqs * res, cm)
    half = group // 2

    def rows_copy(peer, slot, part):
        return res_copy(
            align_ref.at[pl.ds(peer * group + part * half, half)],
            rows.at[pl.ds(part * half, half), pl.ds(pl.multiple_of(slot * res, res), res), :],
            rows_s.at[part, peer], rows_r.at[part, slot], peer,
        )

    def send_rows(part):
        def send(t, c):
            rows_copy(lax.rem(me + t, n_res), me, part).start()
            return c

        lax.fori_loop(1, n_res, send, 0)

    maps[:, : 2 * chan] = dot3(split(normed), split(w_in_ref[...]), ROWS_ROWS)
    source = lax.broadcasted_iota(jnp.int32, (2 * chan, 2 * width), 0)
    column = lax.broadcasted_iota(jnp.int32, (2 * chan, 2 * width), 1)
    placed = jnp.zeros((seqs, 2 * width), F32)
    for r in range(res):
        target = jnp.where(source < chan, source * res + r, width + r * chan + source - chan)
        pick = jnp.where(column == target, 1.0, 0.0).astype(BF16)
        high, low = split(maps[pl.ds(r, seqs, stride=res), :][:, : 2 * chan])
        placed = placed + (dot(high, pick) + dot(low, pick))
    left[chip] = placed[:, :width]
    right[core] = placed[:, width:]
    pl.semaphore_wait(barrier, devices - 1)

    def left_copy(to, slot):
        return res_copy(
            left.at[chip], left.at[slot], left_s.at[to], left_r.at[slot], to * PAIR + core
        )

    def send_left(t, c):
        left_copy(lax.rem(chip + t, chips), chip).start()
        return c

    def right_copy(slot):
        return res_copy(
            right.at[core], right.at[slot], right_s.at[0], right_r.at[0], sibling
        )

    right_copy(core).start()
    lax.fori_loop(1, chips, send_left, 0)

    send_rows(0)
    send_rows(1)
    rows[:, pl.ds(pl.multiple_of(me * res, res), res), :] = align_ref[pl.ds(me * group, group)]

    for load in loads:
        load.wait()
    for ref, wref in ((w_pair, w_out_v), (w_proj, w_project_v), (w_outp, w_output_v)):
        high, low = split(wref[...])
        ref[0] = high
        ref[1] = low

    right_copy(1 - core).wait_recv()
    both = jnp.concatenate([right[k] for k in range(PAIR)], axis=1)
    r_high, r_low = split(both)
    right3[...] = jnp.concatenate([r_high, r_low, r_high], axis=0)
    per = LANES // chan
    lane = lax.broadcasted_iota(jnp.int32, (1, LANES), 1) // chan

    def outer_step(src):
        high, low = split(left[src])
        product = dot(jnp.concatenate([high, high, low], axis=0), right3[...], COLS_COLS)
        parts = product.reshape(chan // per, per, res, PAIR * width)
        blocks = []
        for j in range(PAIR * res):
            base = (j // per) * LANES
            acc = None
            for q in range(per):
                piece = parts[:, q, :, base : base + LANES].reshape(-1, LANES)
                shift = ((q - j % per) * chan) % LANES
                if shift:
                    piece = pltpu.roll(piece, shift, 1)
                acc = piece if acc is None else jnp.where(lane == q, piece, acc)
            blocks.append(
                jnp.concatenate([acc[g * res : (g + 1) * res] for g in range(chan // per)], axis=1)
            )
        flat = jnp.concatenate(blocks, axis=0)
        summed_pair = dot3(
            split(flat), (w_pair[0], w_pair[1])
        )
        for k in range(PAIR):
            update[src, k] = summed_pair[k * part_rows : (k + 1) * part_rows]

    def sum_copy(owner, k, slot_seq, slot_core):
        return any_copy(
            update.at[owner, k], partial.at[slot_seq, slot_core],
            sum_s.at[owner, k], sum_r.at[slot_seq, slot_core], owner, chip * PAIR + k,
        )

    def outer_loop(t, c):
        src = lax.rem(chip + chips - t, chips)
        @pl.when(t > 0)
        def _():
            left_copy(src, src).wait_recv()
        outer_step(src)
        for k in range(PAIR):
            @pl.when(jnp.logical_or(src != my_seq, core != k))
            def _():
                sum_copy(src, k, my_seq, core).start()
        return c

    lax.fori_loop(0, chips, outer_loop, 0)

    def project(s, c):
        parts = split(layer_norm(rows[s], row_gain_ref[...]))
        mapped = dot3(parts, (w_proj[0], w_proj[1]))
        for buf, k in ((q_buf, 0), (k_buf, 1), (v_buf, 2)):
            value = mapped[:, k * cm : (k + 1) * cm]
            if k == 0:
                value = value * head ** (-0.5)
            high, low = split(value)
            buf[0, s] = high
            buf[1, s] = low
        gate[s] = jax.nn.sigmoid(mapped[:, 3 * cm :])
        return c

    def project_part(part):
        def wait_rows(t, c):
            src = lax.rem(me + n_res - t, n_res)
            rows_copy(src, src, part).wait_recv()
            return c

        lax.fori_loop(1, n_res, wait_rows, 0)
        lax.fori_loop(part * half, (part + 1) * half, project, 0)


    partial[my_seq, core] = update[my_seq, core]
    for a in range(n_seq):
        for k in range(PAIR):
            @pl.when(jnp.logical_or(a != my_seq, core != k))
            def _():
                sum_copy(a, k, a, k).wait_recv()
    summed = jnp.concatenate(
        [functools.reduce(jnp.add, [partial[a, k] for a in range(n_seq)]) for k in range(PAIR)],
        axis=0,
    )
    total[...] = summed * (1.0 / (seqs * n_seq))

    lane_row = lax.broadcasted_iota(jnp.int32, (res, heads * row_block), 1) % row_block
    expand_h = lax.broadcasted_iota(jnp.int32, (heads, heads * row_block), 0)
    expand_l = lax.broadcasted_iota(jnp.int32, (heads, heads * row_block), 1)
    expand = jnp.where(expand_l // row_block == expand_h, 1.0, 0.0)
    w_rep = lax.dot_general(
        w_bias_ref[...], expand, COLS_COLS,
        precision=lax.Precision.HIGHEST, preferred_element_type=F32,
    )
    tiles = []
    for i in range(row_block):
        start = (i // res) * res * res + i % res
        tile = pair_ref[i] + total[pl.ds(start, res, stride=res), :]
        pair_out_ref[i] = tile
        tiles.append(layer_norm(tile, pair_gain_ref[...]))
    spread = lax.dot_general(
        jnp.concatenate(tiles, axis=0), w_rep, ROWS_COLS,
        precision=lax.Precision.HIGHEST, preferred_element_type=F32,
    )
    tile_bias = jnp.zeros((res, heads * row_block), F32)
    for i in range(row_block):
        tile_bias = jnp.where(lane_row == i, spread[i * res : (i + 1) * res], tile_bias)
    bias[my_seq, pl.ds(pl.multiple_of(me * res, res), res), :] = tile_bias

    def bias_copy(other, slot):
        place = bias.at[slot // n_res, pl.ds(pl.multiple_of(lax.rem(slot, n_res) * res, res), res)]
        own = bias.at[my_seq, pl.ds(pl.multiple_of(me * res, res), res)]
        return any_copy(
            own, place, bias_s.at[other], bias_r.at[slot], other // n_res, lax.rem(other, n_res)
        )

    def send_bias(t, c):
        bias_copy(lax.rem(mine + t, devices), mine).start()
        return c

    lax.fori_loop(1, devices, send_bias, 0)

    project_part(0)
    project_part(1)

    def wait_bias(t, c):
        src = lax.rem(mine + devices - t, devices)
        bias_copy(src, src).wait_recv()
        return c

    lax.fori_loop(1, devices, wait_bias, 0)

    channel_head = lax.broadcasted_iota(jnp.int32, (row_block, cm), 1) // head

    def out_copy(s, peer, slot, to):
        return res_copy(
            done.at[s, pl.ds(pl.multiple_of(peer * res, res), res)],
            out_ref.at[slot * group + s],
            out_s.at[s, peer], out_r.at[s, slot], to,
        )

    def own_copy(s):
        return pltpu.make_async_copy(
            done.at[s, pl.ds(pl.multiple_of(me * res, res), res)],
            out_ref.at[me * group + s], own_s.at[s],
        )

    def attend(s, c):
        keys = (k_buf[0, s], k_buf[1, s])
        v_high, v_low = v_buf[0, s], v_buf[1, s]
        values3 = jnp.concatenate([v_high, v_low, v_high], axis=0)
        mixed = []
        for a0 in range(0, n_seq, CHUNK):
            chunk = range(a0, min(a0 + CHUNK, n_seq))
            stacked = [
                jnp.concatenate(
                    [jnp.where(channel_head == h, block, jnp.zeros_like(block))
                     for block in [q_buf[k, s, a * row_block : (a + 1) * row_block, :] for a in chunk]
                     for h in range(heads)], axis=0)
                for k in range(2)
            ]
            scores = dot3(keys, stacked, ROWS_ROWS) + jnp.concatenate([bias[a] for a in chunk], axis=1)
            peak = jnp.max(scores, axis=0, keepdims=True)
            powers = jnp.exp(scores - peak)
            weights = powers / jnp.sum(powers, axis=0, keepdims=True)
            p_high, p_low = split(weights)
            blended = dot(jnp.concatenate([p_high, p_high, p_low], axis=0), values3, COLS_COLS)
            for n in range(len(chunk)):
                base = n * heads * row_block
                acc = blended[base : base + row_block]
                for h in range(1, heads):
                    low = base + h * row_block
                    acc = jnp.where(channel_head == h, blended[low : low + row_block], acc)
                mixed.append(acc)
        gated = gate[s] * jnp.concatenate(mixed, axis=0)
        done[s] = rows[s] + dot3(split(gated), (w_outp[0], w_outp[1]))
        own_copy(s).start()

        def send_out(t, d):
            peer = lax.rem(me + t, n_res)
            out_copy(s, peer, me, peer).start()
            return d

        lax.fori_loop(1, n_res, send_out, 0)
        return c

    lax.fori_loop(0, group, attend, 0)

    def finish(t, c):
        src = lax.rem(me + n_res - t, n_res)

        def finish_one(s, d):
            out_copy(s, src, src, src).wait()
            return d

        lax.fori_loop(0, group, finish_one, 0)
        rows_copy(src, src, 0).wait_send()
        rows_copy(src, src, 1).wait_send()
        return c

    lax.fori_loop(1, n_res, finish, 0)

    def finish_own(s, c):
        own_copy(s).wait()
        return c

    lax.fori_loop(0, group, finish_own, 0)

    def finish_left(t, c):
        left_copy(lax.rem(chip + t, chips), chip).wait_send()
        return c

    lax.fori_loop(1, chips, finish_left, 0)
    right_copy(core).wait_send()
    for a in range(n_seq):
        for k in range(PAIR):
            @pl.when(jnp.logical_or(a != my_seq, core != k))
            def _():
                sum_copy(a, k, my_seq, core).wait_send()

    def finish_bias(t, c):
        bias_copy(lax.rem(mine + t, devices), mine).wait_send()
        return c

    lax.fori_loop(1, devices, finish_bias, 0)


def on_device(n_seq, n_res, *args):
    align, pair, _, w_in, w_out, _, w_bias, _, w_project, w_output = args
    seqs, res, cm = align.shape
    row_block, _, cz = pair.shape
    heads = w_bias.shape[1]
    chan = w_in.shape[1] // 2
    assert row_block == PAIR * res and n_res == PAIR * n_seq
    chips = n_res // PAIR
    group = seqs // n_res
    assert group % 2 == 0
    total_res = res * n_res
    width = res * chan
    vmem = pl.BlockSpec(memory_space=pltpu.VMEM)
    dma = pltpu.SemaphoreType.DMA
    scratch = [
        pltpu.VMEM((seqs * res, LANES), F32),
        pltpu.VMEM((chips, seqs, width), F32),
        pltpu.VMEM((PAIR, seqs, width), F32),
        pltpu.VMEM((3 * seqs, PAIR * width), BF16),
        pltpu.VMEM((group, total_res, cm), F32),
        pltpu.VMEM((2,) + w_out.shape, BF16),
        pltpu.VMEM((2,) + w_project.shape, BF16),
        pltpu.VMEM((2,) + w_output.shape, BF16),
        pltpu.VMEM((chips, PAIR, res * res, cz), F32),
        pltpu.VMEM((n_seq, PAIR, res * res, cz), F32),
        pltpu.VMEM((row_block * res, cz), F32),
        pltpu.VMEM((n_seq, total_res, heads * row_block), F32),
        pltpu.VMEM((2, group, total_res, cm), BF16),
        pltpu.VMEM((2, group, total_res, cm), BF16),
        pltpu.VMEM((2, group, total_res, cm), BF16),
        pltpu.VMEM((group, total_res, cm), F32),
        pltpu.VMEM((group, total_res, cm), F32),
        pltpu.VMEM(w_out.shape, F32),
        pltpu.VMEM(w_project.shape, F32),
        pltpu.VMEM(w_output.shape, F32),
        dma((chips,)), dma((chips,)), dma((1,)), dma((1,)), dma((2, n_res)), dma((2, n_res)),
        dma((n_seq, PAIR)), dma((n_seq, PAIR)), dma((n_seq * n_res,)), dma((n_seq * n_res,)),
        dma((group, n_res)), dma((group, n_res)), dma((group,)), dma((3,)),
    ]
    vectors = [a.reshape(1, -1) if a.ndim == 1 else a for a in args]
    vectors[3] = w_in.T
    vectors[6] = w_bias.T
    hbm = pl.BlockSpec(memory_space=pltpu.HBM)
    free = pl.BlockSpec(memory_space=pl.ANY)
    return pl.pallas_call(
        functools.partial(kernel, n_seq, n_res, heads),
        out_shape=(
            jax.ShapeDtypeStruct(align.shape, F32),
            jax.ShapeDtypeStruct(pair.shape, F32),
        ),
        in_specs=[hbm if k in (4, 8, 9) else vmem for k in range(len(args))],
        out_specs=(free, vmem),
        scratch_shapes=scratch,
        compiler_params=pltpu.CompilerParams(
            collective_id=0, has_side_effects=True, vmem_limit_bytes=24 * 1024 * 1024
        ),
    )(*vectors)


def solution(mesh):
    tiled = P("seq", "res", None)
    return jax.shard_map(
        functools.partial(on_device, mesh.shape["seq"], mesh.shape["res"]),
        mesh=mesh,
        in_specs=(tiled, tiled) + (P(),) * 8,
        out_specs=(tiled, tiled),
        check_vma=False,
    )
```

```python
import functools
import jax
import jax.numpy as jnp
from jax import lax
from jax.experimental import pallas as pl
from jax.experimental.pallas import tpu as pltpu
from jax.sharding import PartitionSpec as P

F32 = jnp.float32
BF16 = jnp.bfloat16
MESH = pl.DeviceIdType.MESH
ROWS_COLS = (((1,), (0,)), ((), ()))
ROWS_ROWS = (((1,), (1,)), ((), ()))
COLS_COLS = (((0,), (0,)), ((), ()))
LANES = 128
PAIR = 2
CHUNK = 4


def split(value):
    high = value.astype(BF16)
    low = (value - high.astype(F32)).astype(BF16)
    return high, low


def dot(a, b, dims=ROWS_COLS):
    return lax.dot_general(a, b, dims, preferred_element_type=F32)


def dot3(a, b, dims=ROWS_COLS):
    return dot(a[0], b[0], dims) + (dot(a[0], b[1], dims) + dot(a[1], b[0], dims))


def layer_norm(values, scales):
    average = jnp.mean(values, axis=-1, keepdims=True)
    centered = values - average
    variance = jnp.mean(centered * centered, axis=-1, keepdims=True)
    return centered * lax.rsqrt(variance + 1e-05) * scales


def kernel(
    n_seq, n_res, heads,
    align_ref, pair_ref, outer_gain_ref, w_in_ref, w_out_ref, pair_gain_ref, w_bias_ref,
    row_gain_ref, w_project_ref, w_output_ref,
    out_ref, pair_out_ref,
    maps, left, right, right3, rows, w_pair, w_proj, w_outp, update, partial, total, bias,
    q_buf, k_buf, v_buf, gate, done, w_out_v, w_project_v, w_output_v,
    left_s, left_r, right_s, right_r, rows_s, rows_r, sum_s, sum_r, bias_s, bias_r,
    out_s, out_r, own_s, load_s,
):
    seqs, res, cm = align_ref.shape
    row_block = pair_ref.shape[0]
    cz = pair_ref.shape[2]
    chan = w_in_ref.shape[0] // 2
    group = seqs // n_res
    total_res = res * n_res
    head = cm // heads
    width = res * chan
    devices = n_seq * n_res
    chips = n_res // PAIR
    part_rows = res * res
    my_seq = lax.axis_index("seq")
    me = lax.axis_index("res")

    barrier = pltpu.get_barrier_semaphore()
    mine = my_seq * n_res + me
    core = lax.rem(me, PAIR)
    chip = me // PAIR
    sibling = chip * PAIR + 1 - core

    def greet(t, c):
        other = lax.rem(mine + t, devices)
        pl.semaphore_signal(
            barrier, inc=1, device_id=(other // n_res, lax.rem(other, n_res)), device_id_type=MESH
        )
        return c

    lax.fori_loop(1, devices, greet, 0)
    loads = [
        pltpu.make_async_copy(hbm, held, load_s.at[k])
        for k, (hbm, held) in enumerate(
            ((w_out_ref, w_out_v), (w_project_ref, w_project_v), (w_output_ref, w_output_v))
        )
    ]
    for load in loads:
        load.start()

    def res_copy(src, dst, send, recv, peer):
        return pltpu.make_async_remote_copy(
            src_ref=src, dst_ref=dst, send_sem=send, recv_sem=recv,
            device_id=(my_seq, peer), device_id_type=MESH,
        )

    def any_copy(src, dst, send, recv, seq, peer):
        return pltpu.make_async_remote_copy(
            src_ref=src, dst_ref=dst, send_sem=send, recv_sem=recv,
            device_id=(seq, peer), device_id_type=MESH,
        )

    normed = layer_norm(align_ref[...], outer_gain_ref[...]).reshape(seqs * res, cm)
    half = group // 2

    def rows_copy(peer, slot, part):
        return res_copy(
            align_ref.at[pl.ds(peer * group + part * half, half)],
            rows.at[pl.ds(part * half, half), pl.ds(pl.multiple_of(slot * res, res), res), :],
            rows_s.at[part, peer], rows_r.at[part, slot], peer,
        )

    def send_rows(part):
        def send(t, c):
            rows_copy(lax.rem(me + t, n_res), me, part).start()
            return c

        lax.fori_loop(1, n_res, send, 0)

    maps[:, : 2 * chan] = dot3(split(normed), split(w_in_ref[...]), ROWS_ROWS)
    source = lax.broadcasted_iota(jnp.int32, (2 * chan, 2 * width), 0)
    column = lax.broadcasted_iota(jnp.int32, (2 * chan, 2 * width), 1)
    placed = jnp.zeros((seqs, 2 * width), F32)
    for r in range(res):
        target = jnp.where(source < chan, source * res + r, width + r * chan + source - chan)
        pick = jnp.where(column == target, 1.0, 0.0).astype(BF16)
        high, low = split(maps[pl.ds(r, seqs, stride=res), :][:, : 2 * chan])
        placed = placed + (dot(high, pick) + dot(low, pick))
    left[chip] = placed[:, :width]
    right[core] = placed[:, width:]
    pl.semaphore_wait(barrier, devices - 1)

    def left_copy(to, slot):
        return res_copy(
            left.at[chip], left.at[slot], left_s.at[to], left_r.at[slot], to * PAIR + core
        )

    def send_left(t, c):
        left_copy(lax.rem(chip + t, chips), chip).start()
        return c

    def right_copy(slot):
        return res_copy(
            right.at[core], right.at[slot], right_s.at[0], right_r.at[0], sibling
        )

    right_copy(core).start()
    lax.fori_loop(1, chips, send_left, 0)

    send_rows(0)
    send_rows(1)
    rows[:, pl.ds(pl.multiple_of(me * res, res), res), :] = align_ref[pl.ds(me * group, group)]

    for load in loads:
        load.wait()
    for ref, wref in ((w_pair, w_out_v), (w_proj, w_project_v), (w_outp, w_output_v)):
        high, low = split(wref[...])
        ref[0] = high
        ref[1] = low

    right_copy(1 - core).wait_recv()
    both = jnp.concatenate([right[k] for k in range(PAIR)], axis=1)
    r_high, r_low = split(both)
    right3[...] = jnp.concatenate([r_high, r_low, r_high], axis=0)
    per = LANES // chan
    lane = lax.broadcasted_iota(jnp.int32, (1, LANES), 1) // chan

    def outer_step(src):
        high, low = split(left[src])
        product = dot(jnp.concatenate([high, high, low], axis=0), right3[...], COLS_COLS)
        parts = product.reshape(chan // per, per, res, PAIR * width)
        blocks = []
        for j in range(PAIR * res):
            base = (j // per) * LANES
            acc = None
            for q in range(per):
                piece = parts[:, q, :, base : base + LANES].reshape(-1, LANES)
                shift = ((q - j % per) * chan) % LANES
                if shift:
                    piece = pltpu.roll(piece, shift, 1)
                acc = piece if acc is None else jnp.where(lane == q, piece, acc)
            blocks.append(
                jnp.concatenate([acc[g * res : (g + 1) * res] for g in range(chan // per)], axis=1)
            )
        flat = jnp.concatenate(blocks, axis=0)
        summed_pair = dot3(
            split(flat), (w_pair[0], w_pair[1])
        )
        for k in range(PAIR):
            update[src, k] = summed_pair[k * part_rows : (k + 1) * part_rows]

    def sum_copy(owner, k, slot_seq, slot_core):
        return any_copy(
            update.at[owner, k], partial.at[slot_seq, slot_core],
            sum_s.at[owner, k], sum_r.at[slot_seq, slot_core], owner, chip * PAIR + k,
        )

    def outer_loop(t, c):
        src = lax.rem(chip + chips - t, chips)
        @pl.when(t > 0)
        def _():
            left_copy(src, src).wait_recv()
        outer_step(src)
        for k in range(PAIR):
            @pl.when(jnp.logical_or(src != my_seq, core != k))
            def _():
                sum_copy(src, k, my_seq, core).start()
        return c

    lax.fori_loop(0, chips, outer_loop, 0)

    def project(s, c):
        parts = split(layer_norm(rows[s], row_gain_ref[...]))
        mapped = dot3(parts, (w_proj[0], w_proj[1]))
        for buf, k in ((q_buf, 0), (k_buf, 1), (v_buf, 2)):
            value = mapped[:, k * cm : (k + 1) * cm]
            if k == 0:
                value = value * head ** (-0.5)
            high, low = split(value)
            buf[0, s] = high
            buf[1, s] = low
        gate[s] = jax.nn.sigmoid(mapped[:, 3 * cm :])
        return c

    def project_part(part):
        def wait_rows(t, c):
            src = lax.rem(me + n_res - t, n_res)
            rows_copy(src, src, part).wait_recv()
            return c

        lax.fori_loop(1, n_res, wait_rows, 0)
        for s in range(part * half, (part + 1) * half):
            project(s, 0)


    partial[my_seq, core] = update[my_seq, core]
    for a in range(n_seq):
        for k in range(PAIR):
            @pl.when(jnp.logical_or(a != my_seq, core != k))
            def _():
                sum_copy(a, k, a, k).wait_recv()
    summed = jnp.concatenate(
        [functools.reduce(jnp.add, [partial[a, k] for a in range(n_seq)]) for k in range(PAIR)],
        axis=0,
    )
    total[...] = summed * (1.0 / (seqs * n_seq))

    lane_row = lax.broadcasted_iota(jnp.int32, (res, heads * row_block), 1) % row_block
    expand_h = lax.broadcasted_iota(jnp.int32, (heads, heads * row_block), 0)
    expand_l = lax.broadcasted_iota(jnp.int32, (heads, heads * row_block), 1)
    expand = jnp.where(expand_l // row_block == expand_h, 1.0, 0.0)
    w_rep = lax.dot_general(
        w_bias_ref[...], expand, COLS_COLS,
        precision=lax.Precision.HIGHEST, preferred_element_type=F32,
    )
    tiles = []
    for i in range(row_block):
        start = (i // res) * res * res + i % res
        tile = pair_ref[i] + total[pl.ds(start, res, stride=res), :]
        pair_out_ref[i] = tile
        tiles.append(layer_norm(tile, pair_gain_ref[...]))
    spread = lax.dot_general(
        jnp.concatenate(tiles, axis=0), w_rep, ROWS_COLS,
        precision=lax.Precision.HIGHEST, preferred_element_type=F32,
    )
    tile_bias = jnp.zeros((res, heads * row_block), F32)
    for i in range(row_block):
        tile_bias = jnp.where(lane_row == i, spread[i * res : (i + 1) * res], tile_bias)
    bias[my_seq, pl.ds(pl.multiple_of(me * res, res), res), :] = tile_bias

    def bias_copy(other, slot):
        place = bias.at[slot // n_res, pl.ds(pl.multiple_of(lax.rem(slot, n_res) * res, res), res)]
        own = bias.at[my_seq, pl.ds(pl.multiple_of(me * res, res), res)]
        return any_copy(
            own, place, bias_s.at[other], bias_r.at[slot], other // n_res, lax.rem(other, n_res)
        )

    def send_bias(t, c):
        bias_copy(lax.rem(mine + t, devices), mine).start()
        return c

    lax.fori_loop(1, devices, send_bias, 0)

    project_part(0)
    project_part(1)

    def wait_bias(t, c):
        src = lax.rem(mine + devices - t, devices)
        bias_copy(src, src).wait_recv()
        return c

    lax.fori_loop(1, devices, wait_bias, 0)

    channel_head = lax.broadcasted_iota(jnp.int32, (row_block, cm), 1) // head

    def out_copy(s, peer, slot, to):
        return res_copy(
            done.at[s, pl.ds(pl.multiple_of(peer * res, res), res)],
            out_ref.at[slot * group + s],
            out_s.at[s, peer], out_r.at[s, slot], to,
        )

    def own_copy(s):
        return pltpu.make_async_copy(
            done.at[s, pl.ds(pl.multiple_of(me * res, res), res)],
            out_ref.at[me * group + s], own_s.at[s],
        )

    def attend(s, c):
        keys = (k_buf[0, s], k_buf[1, s])
        v_high, v_low = v_buf[0, s], v_buf[1, s]
        values3 = jnp.concatenate([v_high, v_low, v_high], axis=0)
        mixed = []
        for a0 in range(0, n_seq, CHUNK):
            chunk = range(a0, min(a0 + CHUNK, n_seq))
            stacked = [
                jnp.concatenate(
                    [jnp.where(channel_head == h, block, jnp.zeros_like(block))
                     for block in [q_buf[k, s, a * row_block : (a + 1) * row_block, :] for a in chunk]
                     for h in range(heads)], axis=0)
                for k in range(2)
            ]
            scores = dot3(keys, stacked, ROWS_ROWS) + jnp.concatenate([bias[a] for a in chunk], axis=1)
            peak = jnp.max(scores, axis=0, keepdims=True)
            powers = jnp.exp(scores - peak)
            weights = powers / jnp.sum(powers, axis=0, keepdims=True)
            p_high, p_low = split(weights)
            blended = dot(jnp.concatenate([p_high, p_high, p_low], axis=0), values3, COLS_COLS)
            for n in range(len(chunk)):
                base = n * heads * row_block
                acc = blended[base : base + row_block]
                for h in range(1, heads):
                    low = base + h * row_block
                    acc = jnp.where(channel_head == h, blended[low : low + row_block], acc)
                mixed.append(acc)
        gated = gate[s] * jnp.concatenate(mixed, axis=0)
        done[s] = rows[s] + dot3(split(gated), (w_outp[0], w_outp[1]))
        own_copy(s).start()

        def send_out(t, d):
            peer = lax.rem(me + t, n_res)
            out_copy(s, peer, me, peer).start()
            return d

        lax.fori_loop(1, n_res, send_out, 0)
        return c

    lax.fori_loop(0, group, attend, 0)

    def finish(t, c):
        src = lax.rem(me + n_res - t, n_res)

        def finish_one(s, d):
            out_copy(s, src, src, src).wait()
            return d

        lax.fori_loop(0, group, finish_one, 0)
        rows_copy(src, src, 0).wait_send()
        rows_copy(src, src, 1).wait_send()
        return c

    lax.fori_loop(1, n_res, finish, 0)

    def finish_own(s, c):
        own_copy(s).wait()
        return c

    lax.fori_loop(0, group, finish_own, 0)

    def finish_left(t, c):
        left_copy(lax.rem(chip + t, chips), chip).wait_send()
        return c

    lax.fori_loop(1, chips, finish_left, 0)
    right_copy(core).wait_send()
    for a in range(n_seq):
        for k in range(PAIR):
            @pl.when(jnp.logical_or(a != my_seq, core != k))
            def _():
                sum_copy(a, k, my_seq, core).wait_send()

    def finish_bias(t, c):
        bias_copy(lax.rem(mine + t, devices), mine).wait_send()
        return c

    lax.fori_loop(1, devices, finish_bias, 0)


def on_device(n_seq, n_res, *args):
    align, pair, _, w_in, w_out, _, w_bias, _, w_project, w_output = args
    seqs, res, cm = align.shape
    row_block, _, cz = pair.shape
    heads = w_bias.shape[1]
    chan = w_in.shape[1] // 2
    assert row_block == PAIR * res and n_res == PAIR * n_seq
    chips = n_res // PAIR
    group = seqs // n_res
    assert group % 2 == 0
    total_res = res * n_res
    width = res * chan
    vmem = pl.BlockSpec(memory_space=pltpu.VMEM)
    dma = pltpu.SemaphoreType.DMA
    scratch = [
        pltpu.VMEM((seqs * res, LANES), F32),
        pltpu.VMEM((chips, seqs, width), F32),
        pltpu.VMEM((PAIR, seqs, width), F32),
        pltpu.VMEM((3 * seqs, PAIR * width), BF16),
        pltpu.VMEM((group, total_res, cm), F32),
        pltpu.VMEM((2,) + w_out.shape, BF16),
        pltpu.VMEM((2,) + w_project.shape, BF16),
        pltpu.VMEM((2,) + w_output.shape, BF16),
        pltpu.VMEM((chips, PAIR, res * res, cz), F32),
        pltpu.VMEM((n_seq, PAIR, res * res, cz), F32),
        pltpu.VMEM((row_block * res, cz), F32),
        pltpu.VMEM((n_seq, total_res, heads * row_block), F32),
        pltpu.VMEM((2, group, total_res, cm), BF16),
        pltpu.VMEM((2, group, total_res, cm), BF16),
        pltpu.VMEM((2, group, total_res, cm), BF16),
        pltpu.VMEM((group, total_res, cm), F32),
        pltpu.VMEM((group, total_res, cm), F32),
        pltpu.VMEM(w_out.shape, F32),
        pltpu.VMEM(w_project.shape, F32),
        pltpu.VMEM(w_output.shape, F32),
        dma((chips,)), dma((chips,)), dma((1,)), dma((1,)), dma((2, n_res)), dma((2, n_res)),
        dma((n_seq, PAIR)), dma((n_seq, PAIR)), dma((n_seq * n_res,)), dma((n_seq * n_res,)),
        dma((group, n_res)), dma((group, n_res)), dma((group,)), dma((3,)),
    ]
    vectors = [a.reshape(1, -1) if a.ndim == 1 else a for a in args]
    vectors[3] = w_in.T
    vectors[6] = w_bias.T
    hbm = pl.BlockSpec(memory_space=pltpu.HBM)
    return pl.pallas_call(
        functools.partial(kernel, n_seq, n_res, heads),
        out_shape=(
            jax.ShapeDtypeStruct(align.shape, F32),
            jax.ShapeDtypeStruct(pair.shape, F32),
        ),
        in_specs=[hbm if k in (4, 8, 9) else vmem for k in range(len(args))],
        out_specs=(vmem, vmem),
        scratch_shapes=scratch,
        compiler_params=pltpu.CompilerParams(
            collective_id=0, has_side_effects=True, vmem_limit_bytes=60 * 1024 * 1024
        ),
    )(*vectors)


def solution(mesh):
    tiled = P("seq", "res", None)
    return jax.shard_map(
        functools.partial(on_device, mesh.shape["seq"], mesh.shape["res"]),
        mesh=mesh,
        in_specs=(tiled, tiled) + (P(),) * 8,
        out_specs=(tiled, tiled),
        check_vma=False,
    )
```
